32 devices in a mesh: leaf: 4 (over z), row: 2 (over x), top: 4 (over y, core).
Axes of the slice: x: 2, y: 2, z: 4, core: 2. Of those that a mesh axis runs over, the one named last changes fastest.
Arguments:
- loads: bfloat16 [4, 2, 4, 1, 256, 32], P('leaf', 'row', 'top'), may hold values from -6 to 6
- flux_maps: bfloat16 [4, 2, 4, 640, 256], P('leaf', 'row', 'top'), may hold values from -0.375 to 0.375
- chain_maps: float32 [4, 2, 4, 640, 640], P('leaf', 'row', 'top')
- leaf_maps: bfloat16 [4, 2, 4, 1, 256, 256], P('leaf', 'row', 'top'), may hold values from -0.375 to 0.375
- edge_maps: bfloat16 [4, 2, 4, 1, 256, 640], P('leaf', 'row', 'top'), may hold values from -0.25 to 0.25
- top_maps: bfloat16 [4, 2, 4, 1, 256, 128], P('leaf', 'row', 'top'), may hold values from -0.5 to 0.5
- slot_nodes: int32 [4, 2, 4, 128], P('leaf', 'row', 'top'), may hold values from 0 to 8191
- slot_counts: int32 [4, 2, 4], P('leaf', 'row', 'top'), may hold values from 1 to 128, 320 in all within a row
- top_loads: float32 [8192, 32], P('leaf'), may hold values from -6 to 6
- top_inverse: float32 [8192, 8192], P('top', ('leaf', 'row')), may hold values from -0.0625 to 0.0625
Outputs:
- solution: bfloat16 [4, 2, 4, 1, 256, 32], P('leaf', 'row', 'top')
- top_values: float32 [8192, 32], P('top')
The draws below stay inside these ranges and needn't reach their ends.
Inputs may be any that keep to these rules, and one draw needn't show every extreme that they name: `slot_counts`: over the 4 subtrees of one x-y cell (same x and y, all t) the live slots sum to 320, and one of those subtrees has all 128 slots live.
All inputs are finite; a program needn't handle non-finite values. No bound on the sum of `slot_counts` on one device may be relied on, other than what follows from the above.
Results may differ from the reference program's by a relative error of at most 0.0046.
Values sent between devices are 32-bit elements; how exact they have to be, the bound alone decides.
A program may use at most 64 MiB of HBM per device.

```python
import math
import jax
import jax.numpy as jnp
import numpy as np
from jax import lax

NODES = 256
K = 640
CAP = 128
NRHS = 32
LD = 1
SEP = 8192
SUBTREES_ALONG_X = 4
GY = 2
GT = 4


def draw_chain_maps(key, part):
    random_key_list = jax.random.split(jax.random.fold_in(key, 11), 4)
    share = 0.5
    slow_mask = jax.random.uniform(random_key_list[0], (K,)) < share
    slow_rate = 0.25 ** (1.0 / SUBTREES_ALONG_X)
    jitter = jax.random.uniform(random_key_list[1], (SUBTREES_ALONG_X, GY, GT, K), minval=0.5, maxval=1.0)
    rates = jnp.where(slow_mask, 1.0 - (1.0 - slow_rate) * jitter, 0.6 * jitter)
    explode_position = jax.random.randint(random_key_list[2], (2,), 0, SUBTREES_ALONG_X)
    exploding_rows = jnp.any(jnp.arange(SUBTREES_ALONG_X)[:, None] == explode_position[None, :], axis=1)
    rates = rates * jnp.where(exploding_rows[:, None, None, None] & slow_mask, 0.65, 1.0)
    noise = jax.random.normal(random_key_list[3], (SUBTREES_ALONG_X, GY, GT, K, K), jnp.float32) * (0.2 / K ** 0.5)
    merged = rates[..., None] * (jnp.eye(K, dtype=jnp.float32) + noise)
    return merged.astype(jnp.float32)


def plant(drawn, rng, smallest, largest):
    longest = drawn.shape.index(max(drawn.shape))
    spots = []
    for shift in (0, 1):
        where = [jax.random.randint(jax.random.fold_in(rng, axis), (), 0, length) for axis, length in enumerate(drawn.shape)]
        where[longest] = (where[longest] + shift) % drawn.shape[longest]
        spots.append(tuple(where))
    return drawn.at[spots[0]].set(smallest).at[spots[1]].set(largest)


def block_levels(key, shape, shards, smallest, largest):
    gain = 1.0
    for position, shards_of in shards:
        heights = jax.random.uniform(jax.random.fold_in(jax.random.fold_in(key, 6), position), (shards_of,), jnp.float32, smallest / len(shards), largest / len(shards))
        gain = gain * jnp.repeat(jnp.exp(heights), shape[position] // shards_of).reshape((-1,) + (1,) * (len(shape) - 1 - position))
    return gain


def profile(amount, total, most, slope):
    weights = [(1 << 20) // math.isqrt(standing ** slope) + 1 for standing in range(2, amount + 1)]
    spare, counts = total - most - (amount - 1), [1] * (amount - 1)
    while spare > 0:
        movable = [i for i in range(amount - 1) if counts[i] < most]
        mass, budget = sum([weights[i] for i in movable]), spare
        for i in movable:
            more = min(most - counts[i], max(1, budget * weights[i] // mass), spare)
            counts[i] = counts[i] + more
            spare = spare - more
    return np.array([most] + counts)


def ragged_sizes(stream_key, number_of, total, limit, slope):
    if number_of == 2:
        one = jax.random.randint(stream_key, (), max(1, total - limit), min(limit, total - 1) + 1)
        return jnp.stack([one, total - one])
    tallies = jnp.asarray(profile(number_of, total, limit, slope), jnp.int32)
    pairs = (number_of - 1) // 2
    source_of, receiver = tallies[1:1 + 2 * pairs:2], tallies[2:2 + 2 * pairs:2]
    room = jnp.minimum(source_of - 1, limit - receiver)
    moved = jax.random.randint(jax.random.fold_in(stream_key, 1), (pairs,), 0, 1 << 20) % (room + 1)
    tallies = tallies.at[1:1 + 2 * pairs:2].set(source_of - moved).at[2:2 + 2 * pairs:2].set(receiver + moved)
    return tallies[jax.random.permutation(jax.random.fold_in(stream_key, 2), number_of)]


def centred(stream_key, shape, width, bound, cuts=(), kind=jnp.bfloat16):
    factor_of = block_levels(stream_key, shape, cuts, -0.22, 0.18) if cuts else 1.0
    values = jax.random.normal(stream_key, shape, jnp.float32) * width * factor_of
    return jnp.minimum(jnp.maximum(values, -bound), bound).astype(kind)


def setup_inputs(seed: int = 0) -> dict:
    key_of = jax.random.split(jax.random.key(seed), 11)
    loads = centred(key_of[0], (SUBTREES_ALONG_X, GY, GT, LD, NODES, NRHS), 1.0, 6.0, ((0, 4), (1, 2), (2, 4)))
    flux_maps = centred(key_of[1], (SUBTREES_ALONG_X, GY, GT, K, LD * NODES), (LD * NODES) ** -0.5, 0.375, ((0, 4), (1, 2), (2, 4)))
    chain_maps = draw_chain_maps(jax.random.fold_in(key_of[10], 71), 0)
    leaf_maps = centred(key_of[3], (SUBTREES_ALONG_X, GY, GT, LD, NODES, NODES), NODES ** -0.5, 0.375, ((0, 4), (1, 2), (2, 4)))
    edge_maps = centred(key_of[4], (SUBTREES_ALONG_X, GY, GT, LD, NODES, K), K ** -0.5, 0.25, ((0, 4), (1, 2), (2, 4)))
    top_maps = centred(key_of[5], (SUBTREES_ALONG_X, GY, GT, LD, NODES, CAP), CAP ** -0.5, 0.5, ((0, 4), (1, 2), (2, 4)))
    slot_nodes = plant(jax.random.randint(key_of[6], (SUBTREES_ALONG_X, GY, GT, CAP), 0, SEP), jax.random.fold_in(key_of[6], 1), 0, SEP - 1).astype(jnp.int32)
    slot_counts = jax.vmap(lambda own: ragged_sizes(own, GT, GT * CAP * 5 // 8, CAP, 2))(jax.random.split(key_of[7], SUBTREES_ALONG_X * GY)).reshape((SUBTREES_ALONG_X, GY, GT)).astype(jnp.int32)
    top_loads = centred(key_of[8], (SEP, NRHS), 1.0, 6.0, ((0, 4),), jnp.float32)
    top_inverse = centred(key_of[9], (SEP, SEP), (SEP * (1 + SUBTREES_ALONG_X * GY * GT * CAP // SEP)) ** -0.5, 0.0625, ((0, 4), (1, 8)), jnp.float32)
    return dict(loads=loads, flux_maps=flux_maps, chain_maps=chain_maps, leaf_maps=leaf_maps, edge_maps=edge_maps, top_maps=top_maps, slot_nodes=slot_nodes, slot_counts=slot_counts, top_loads=top_loads, top_inverse=top_inverse)


def reference(loads, flux_maps, chain_maps, leaf_maps, edge_maps, top_maps, slot_nodes, slot_counts, top_loads, top_inverse):
    flattened = loads.reshape(SUBTREES_ALONG_X, GY, GT, LD * NODES, NRHS).astype(jnp.float32)
    fluxes = jnp.einsum("abckn,abcnr->abckr", flux_maps.astype(jnp.float32), flattened)

    def advance_state(before_state, pair):
        combine_operator, flux_part = pair
        after_state = jnp.einsum("gtkj,gtjr->gtkr", combine_operator, before_state, precision=lax.Precision.HIGHEST) + flux_part
        return after_state, after_state

    start_state = jnp.zeros((GY, GT, K, NRHS), jnp.float32)
    _, states = lax.scan(advance_state, start_state, (chain_maps, fluxes))
    edge_rows = states[:, :, :, :CAP, :]
    is_live = jnp.arange(CAP, dtype=jnp.int32)[None, None, None, :] < slot_counts[..., None]
    chosen_entries = jnp.where(is_live[..., None], edge_rows, jnp.float32(0.0))
    top_sum = jax.ops.segment_sum(chosen_entries.reshape(-1, NRHS), slot_nodes.reshape(-1).astype(jnp.int32), num_segments=SEP)
    top_rhs = top_loads - top_sum
    top_values = jnp.dot(top_inverse, top_rhs, precision=lax.Precision.HIGHEST, preferred_element_type=jnp.float32)
    boundary = jnp.where(is_live[..., None], top_values[slot_nodes.astype(jnp.int32)], jnp.float32(0.0))
    states_low = states.astype(jnp.bfloat16).astype(jnp.float32)
    boundary_low = boundary.astype(jnp.bfloat16).astype(jnp.float32)
    summed = jnp.einsum("abclij,abcljr->abclir", leaf_maps.astype(jnp.float32), loads.astype(jnp.float32))
    summed = summed + jnp.einsum("abclik,abckr->abclir", edge_maps.astype(jnp.float32), states_low)
    summed = summed + jnp.einsum("abclis,abcsr->abclir", top_maps.astype(jnp.float32), boundary_low)
    return summed.astype(jnp.bfloat16), top_values
```

```python
import functools

import jax
import jax.numpy as jnp
from jax import lax
from jax.experimental import pallas as pl
from jax.experimental.pallas import tpu as pltpu
from jax.sharding import PartitionSpec as P

LANES = 128
MESH = pl.DeviceIdType.MESH


def nt(a, b):
    return lax.dot_general(a, b, (((1,), (1,)), ((), ())), preferred_element_type=jnp.float32)


def split(value):
    high = value.astype(jnp.bfloat16)
    low = (value - high.astype(jnp.float32)).astype(jnp.bfloat16)
    return high, low


def fold(value):
    half = value.shape[0] // 2
    return value[:half] + value[half:]


def fused_kernel(
    sizes,
    loads_ref,
    ids_ref,
    top_loads_ref,
    flux_hbm,
    chain_hbm,
    leaf_hbm,
    edge_hbm,
    top_hbm,
    inverse_hbm,
    solution_ref,
    values_ref,
    flux_maps,
    chain,
    leaf_maps,
    edge_maps,
    top_maps,
    inverse,
    chain_high,
    chain_low,
    inverse_high,
    inverse_low,
    fluxes,
    state,
    carry,
    early,
    ids,
    entries,
    scatter_table,
    gather_table,
    rhs,
    partials,
    arrived,
    values,
    picked,
    boundary,
    load_sem,
    carry_sem,
    id_leaf_send,
    id_leaf_recv,
    id_cell_send,
    id_cell_recv,
    entry_leaf_send,
    entry_leaf_recv,
    entry_cell_send,
    entry_cell_recv,
    part_send,
    part_recv,
    value_send,
    value_recv,
    bound_send,
    bound_recv,
):
    L, R, T = sizes
    cells, owners = R * T, L * R
    leaf, row, top = lax.axis_index("leaf"), lax.axis_index("row"), lax.axis_index("top")
    cell = row * T + top
    owner = leaf * R + row
    nrhs = loads_ref.shape[0]
    slots = ids_ref.shape[1]
    chunk = inverse.shape[0] // owners
    columns = inverse.shape[1]
    block_rows = inverse.shape[0]

    def along(start, size):
        return pl.ds(pl.multiple_of(start * size, size), size)

    def send(src, dst, send_sem, recv_sem, where):
        return pltpu.make_async_remote_copy(
            src_ref=src,
            dst_ref=dst,
            send_sem=send_sem,
            recv_sem=recv_sem,
            device_id=where,
            device_id_type=MESH,
        )

    def cell_of(step):
        other = lax.rem(cell + step, cells)
        return other, {"row": other // T, "top": lax.rem(other, T)}

    def owner_of(step):
        other = lax.rem(owner + step, owners)
        return other, {"leaf": other // R, "row": lax.rem(other, R)}

    def leaf_of(step):
        other = lax.rem(leaf + step, L)
        return other, {"leaf": other}

    def top_of(step):
        other = lax.rem(top + step, T)
        return other, {"top": other}

    pairs = (
        (flux_hbm, flux_maps),
        (chain_hbm, chain),
        (inverse_hbm, inverse),
        (leaf_hbm, leaf_maps),
        (edge_hbm, edge_maps),
        (top_hbm, top_maps),
    )
    fetches = [
        pltpu.make_async_copy(src, dst, load_sem.at[i]) for i, (src, dst) in enumerate(pairs)
    ]
    for fetch in fetches:
        fetch.start()

    barrier = pltpu.get_barrier_semaphore()
    for step in range(1, cells):
        pl.semaphore_signal(barrier, inc=1, device_id=cell_of(step)[1], device_id_type=MESH)
    for step in range(1, owners):
        pl.semaphore_signal(barrier, inc=1, device_id=owner_of(step)[1], device_id_type=MESH)
    pl.semaphore_wait(barrier, cells + owners - 2)

    mine = cell * L + leaf
    id_copies = [
        send(
            ids_ref,
            ids.at[:, along(mine, slots)],
            id_leaf_send.at[step - 1],
            id_leaf_recv.at[step - 1],
            leaf_of(step)[1],
        )
        for step in range(1, L)
    ]
    for copy in id_copies:
        copy.start()
    ids[:, along(mine, slots)] = ids_ref[...]

    fetches[0].wait()
    fluxes[...] = nt(loads_ref[...], flux_maps[...])
    state[...] = fluxes[...]

    for copy in id_copies:
        copy.wait()
    id_cells = [
        send(
            ids.at[:, along(cell, L * slots)],
            ids.at[:, along(cell, L * slots)],
            id_cell_send.at[step - 1],
            id_cell_recv.at[step - 1],
            cell_of(step)[1],
        )
        for step in range(1, cells)
    ]
    for copy in id_cells:
        copy.start()

    fetches[1].wait()

    @pl.when(leaf > 0)
    def _():
        high, low = split(chain[...])
        chain_high[...] = high
        chain_low[...] = low

    for copy in id_cells:
        copy.wait()

    def prepare():
        @pl.loop(0, columns // 32)
        def _(i):
            start = pl.multiple_of(i * 32, 32)
            numbers = lax.broadcasted_iota(jnp.int32, (32, ids.shape[1]), 0)
            hit = (numbers + (owner * columns + start)) == ids[0:1, :]
            scatter_table[pl.ds(start, 32), :] = jnp.where(hit, 1.0, 0.0).astype(jnp.bfloat16)

        @pl.loop(0, block_rows // 64)
        def _(i):
            start = pl.multiple_of(i * 64, 64)
            numbers = lax.broadcasted_iota(jnp.int32, (64, slots), 0) + (top * block_rows + start)
            for other in range(T):
                wanted = ids[0:1, along((row * T + other) * L + leaf, slots)]
                gather_table[pl.ds(start, 64), other * slots : (other + 1) * slots] = jnp.where(
                    numbers == wanted, 1.0, 0.0
                ).astype(jnp.bfloat16)

        fetches[2].wait()

        @pl.loop(0, block_rows // 64)
        def _(i):
            start = pl.multiple_of(i * 64, 64)
            high, low = split(inverse[pl.ds(start, 64), :])
            inverse_high[pl.ds(start, 64), :] = high
            inverse_low[pl.ds(start, 64), :] = low

    def entry_leaf(step):
        return send(
            state.at[:, pl.ds(0, slots)],
            entries.at[:, along(mine, slots)],
            entry_leaf_send.at[step - 1],
            entry_leaf_recv.at[leaf],
            leaf_of(step)[1],
        )

    def entry_landed(source):
        return pltpu.make_async_copy(
            entries.at[:, along(cell * L + source, slots)],
            entries.at[:, along(cell * L + source, slots)],
            entry_leaf_recv.at[source],
        )

    def entry_cell(source, step):
        number = cell * L + source
        return send(
            entries.at[:, along(number, slots)],
            entries.at[:, along(number, slots)],
            entry_cell_send.at[source * cells + step],
            entry_cell_recv.at[number],
            cell_of(step)[1],
        )

    next_carry = send(state, carry, carry_sem.at[0], carry_sem.at[1], leaf_of(1)[1])

    def forward(source):
        @pl.when(leaf != source)
        def _():
            entry_landed(source).wait()

        for step in range(1, cells):
            entry_cell(source, step).start()

    @pl.loop(0, L)
    def _(k):
        @pl.when(leaf == k)
        def _():
            @pl.when(k > 0)
            def _():
                next_carry.wait_recv()
                high, low = split(carry[...])
                both = jnp.concatenate([high, low], axis=0)
                state[...] = (
                    fluxes[...] + fold(nt(both, chain_high[...])) + nt(high, chain_low[...])
                )

            @pl.when(k < L - 1)
            def _():
                next_carry.start()

            for step in range(1, L):
                entry_leaf(step).start()
            entries[:, along(mine, slots)] = state[:, :slots]

        @pl.when(k > 0)
        def _():
            forward(k - 1)

        @pl.when(lax.rem(leaf + L // 2, L) == k)
        def _():
            prepare()

    forward(L - 1)

    fetches[3].wait()
    fetches[4].wait()
    fetches[5].wait()
    early[...] = nt(loads_ref[...], leaf_maps[...]) + nt(
        state[...].astype(jnp.bfloat16), edge_maps[...]
    )

    @pl.when(leaf < L - 1)
    def _():
        next_carry.wait_send()

    for step in range(1, L):
        entry_leaf(step).wait_send()

    for step in range(1, cells):
        other, _ = cell_of(step)
        for source in range(L):
            number = other * L + source
            pltpu.make_async_copy(
                entries.at[:, along(number, slots)],
                entries.at[:, along(number, slots)],
                entry_cell_recv.at[number],
            ).wait()

    high, low = split(entries[...])
    both = jnp.concatenate([high, low], axis=0)
    width = 256

    @pl.loop(0, columns // width)
    def _(i):
        start = pl.multiple_of(i * width, width)
        total = fold(nt(both, scatter_table[pl.ds(start, width), :]))
        here = top_loads_ref[:, pl.ds(pl.multiple_of(row * columns + start, width), width)]
        high, low = split(here - total)
        rhs[0:nrhs, pl.ds(start, width)] = high
        rhs[nrhs : 2 * nrhs, pl.ds(start, width)] = low

    def product(number):
        rows = along(number, chunk)
        return fold(nt(rhs[...], inverse_high[rows, :])) + nt(rhs[0:nrhs, :], inverse_low[rows, :])

    def part_copy(step):
        where = owner_of(step)[1]
        return send(
            partials.at[step],
            arrived.at[step],
            part_send.at[step],
            part_recv.at[step],
            where,
        )

    @pl.loop(1, owners)
    def _(step):
        partials[step] = product(owner_of(step)[0])
        part_copy(step).start()

    total = product(owner)
    for step in range(1, owners):
        part_copy(step).wait_recv()
        total = total + arrived[step]
    values[:, along(owner, chunk)] = total

    def value_copy(step):
        where = owner_of(step)[1]
        return send(
            values.at[:, along(owner, chunk)],
            values.at[:, along(owner, chunk)],
            value_send.at[step],
            value_recv.at[step],
            where,
        )

    for step in range(1, owners):
        value_copy(step).start()
    for step in range(1, owners):
        part_copy(step).wait_send()
    for step in range(1, owners):
        value_copy(step).wait_recv()

    final = values[...]
    values_ref[...] = final
    gathered = jnp.dot(
        final.astype(jnp.bfloat16), gather_table[...], preferred_element_type=jnp.float32
    )
    for other in range(T):
        picked[other] = gathered[:, other * slots : (other + 1) * slots]

    def bound_copy(step):
        other, where = top_of(step)
        return send(
            picked.at[other], boundary.at[step], bound_send.at[step], bound_recv.at[step], where
        )

    for step in range(1, T):
        bound_copy(step).start()
    bound = picked[top]
    for step in range(1, T):
        bound_copy(step).wait_recv()
        bound = bound + boundary[step]
    late = nt(bound.astype(jnp.bfloat16), top_maps[...])
    solution_ref[...] = (early[...] + late).astype(jnp.bfloat16)

    for source in range(L):
        for step in range(1, cells):
            entry_cell(source, step).wait_send()
    for step in range(1, owners):
        value_copy(step).wait_send()
    for step in range(1, T):
        bound_copy(step).wait_send()


def fused_body(
    sizes,
    loads,
    flux_maps,
    chain_maps,
    leaf_maps,
    edge_maps,
    top_maps,
    slot_nodes,
    slot_counts,
    top_loads,
    top_inverse,
):
    L, R, T = sizes
    cells, owners = R * T, L * R
    node_count, nrhs = loads.shape[4:]
    sep_width = chain_maps.shape[-1]
    slots = slot_nodes.shape[-1]
    block_rows, columns = top_inverse.shape
    chunk = block_rows // owners
    everyone = L * cells
    f32, bf16 = jnp.float32, jnp.bfloat16
    nodes = slot_nodes.reshape(1, slots)
    live = lax.broadcasted_iota(jnp.int32, (8, slots), 1) < slot_counts.reshape(1, 1)
    ids = jnp.where(live, nodes, -1)
    dma = pltpu.SemaphoreType.DMA
    vmem = pl.BlockSpec(memory_space=pltpu.VMEM)
    anywhere = pl.BlockSpec(memory_space=pl.ANY)
    solution, values = pl.pallas_call(
        functools.partial(fused_kernel, sizes),
        out_shape=(
            jax.ShapeDtypeStruct((nrhs, node_count), bf16),
            jax.ShapeDtypeStruct((nrhs, block_rows), f32),
        ),
        in_specs=[vmem] * 3 + [anywhere] * 6,
        out_specs=(vmem, vmem),
        scratch_shapes=[
            pltpu.VMEM((sep_width, node_count), bf16),
            pltpu.VMEM((sep_width, sep_width), f32),
            pltpu.VMEM((node_count, node_count), bf16),
            pltpu.VMEM((node_count, sep_width), bf16),
            pltpu.VMEM((node_count, slots), bf16),
            pltpu.VMEM((block_rows, columns), f32),
            pltpu.VMEM((sep_width, sep_width), bf16),
            pltpu.VMEM((sep_width, sep_width), bf16),
            pltpu.VMEM((block_rows, columns), bf16),
            pltpu.VMEM((block_rows, columns), bf16),
            pltpu.VMEM((nrhs, sep_width), f32),
            pltpu.VMEM((nrhs, sep_width), f32),
            pltpu.VMEM((nrhs, sep_width), f32),
            pltpu.VMEM((nrhs, node_count), f32),
            pltpu.VMEM((8, everyone * slots), jnp.int32),
            pltpu.VMEM((nrhs, everyone * slots), f32),
            pltpu.VMEM((columns, everyone * slots), bf16),
            pltpu.VMEM((block_rows, T * slots), bf16),
            pltpu.VMEM((2 * nrhs, columns), bf16),
            pltpu.VMEM((owners, nrhs, chunk), f32),
            pltpu.VMEM((owners, nrhs, chunk), f32),
            pltpu.VMEM((nrhs, block_rows), f32),
            pltpu.VMEM((T, nrhs, slots), f32),
            pltpu.VMEM((T, nrhs, slots), f32),
            dma((6,)),
            dma((2,)),
            dma((L,)),
            dma((L,)),
            dma((cells,)),
            dma((cells,)),
            dma((L,)),
            dma((L,)),
            dma((everyone,)),
            dma((everyone,)),
            dma((owners,)),
            dma((owners,)),
            dma((owners,)),
            dma((owners,)),
            dma((T,)),
            dma((T,)),
        ],
        compiler_params=pltpu.CompilerParams(
            collective_id=0, has_side_effects=True, vmem_limit_bytes=56 << 20
        ),
    )(
        loads.reshape(node_count, nrhs).T,
        ids,
        top_loads.T,
        flux_maps.reshape(sep_width, node_count),
        chain_maps.reshape(sep_width, sep_width),
        leaf_maps.reshape(node_count, node_count),
        edge_maps.reshape(node_count, sep_width),
        top_maps.reshape(node_count, slots),
        top_inverse,
    )
    return solution.T.reshape(1, 1, 1, 1, node_count, nrhs), values.T


def fits(sizes, loads, chain_maps, slot_nodes, top_loads, top_inverse):
    L, R, T = sizes
    owners = L * R
    block_rows, columns = top_inverse.shape
    slots = slot_nodes.shape[-1]
    everyone = owners * T * slots
    return (
        min(sizes) > 1
        and loads.shape[3] == 1
        and loads.shape[5] % 16 == 0
        and slots == LANES
        and chain_maps.shape[-1] % LANES == 0
        and loads.shape[4] % LANES == 0
        and columns % 256 == 0
        and block_rows % (owners * LANES) == 0
        and top_loads.shape[0] == R * columns
        and columns * everyone * 2 + block_rows * columns * 8 < (32 << 20)
    )


def passed_along(value, axis, steps):
    count = lax.axis_size(axis)
    first, last = (max(0, -steps), min(count, count - steps))
    return lax.ppermute(value, axis, [(source, source + steps) for source in range(first, last)])


def plain_body(
    loads,
    flux_maps,
    chain_maps,
    leaf_maps,
    edge_maps,
    top_maps,
    slot_nodes,
    slot_counts,
    top_loads,
    top_inverse,
):
    leaf_count = loads.shape[3]
    node_count = loads.shape[4]
    rhs_count = loads.shape[5]
    sep_width = chain_maps.shape[-1]
    slot_total = slot_nodes.shape[-1]
    largest_level = lax.Precision.HIGHEST
    local_loads = loads.reshape(leaf_count, node_count, rhs_count)
    flattened = loads.reshape(leaf_count * node_count, rhs_count)
    fluxes = jnp.dot(
        flux_maps.reshape(sep_width, leaf_count * node_count),
        flattened,
        preferred_element_type=jnp.float32,
    )
    combine_operator = chain_maps.reshape(sep_width, sep_width)
    chain_index = lax.axis_index("leaf")

    def advance(step_index, carried):
        earlier = passed_along(carried, "leaf", 1)
        advanced = (
            jnp.dot(
                combine_operator,
                earlier,
                precision=largest_level,
                preferred_element_type=jnp.float32,
            )
            + fluxes
        )
        return jnp.where(chain_index == step_index, advanced, carried)

    states = lax.fori_loop(1, lax.axis_size("leaf"), advance, fluxes)
    slot_ids = slot_nodes.reshape(slot_total)
    is_live = lax.iota(jnp.int32, slot_total) < slot_counts.reshape(())
    chosen_entries = jnp.where(is_live[:, None], states[:slot_total], jnp.float32(0.0))
    block_rows = top_loads.shape[0]
    row_ids = lax.iota(jnp.int32, block_rows * lax.axis_size("leaf"))
    match_table = (row_ids[:, None] == slot_ids[None, :]).astype(jnp.float32)
    top_block = lax.psum_scatter(
        jnp.dot(
            match_table, chosen_entries, precision=largest_level, preferred_element_type=jnp.float32
        ),
        "leaf",
        scatter_dimension=0,
        tiled=True,
    )
    top_block = lax.psum(top_block, ("row", "top"))
    rhs_block = top_loads - top_block
    column_rows = top_inverse.shape[1]
    rhs_piece = lax.dynamic_slice_in_dim(
        rhs_block, lax.axis_index("row") * column_rows, column_rows, 0
    )
    partial_value = jnp.dot(
        top_inverse, rhs_piece, precision=largest_level, preferred_element_type=jnp.float32
    )
    owned_rows = lax.psum(partial_value, ("leaf", "row"))
    shard_piece = lax.all_gather(owned_rows, "top", axis=0, tiled=True)
    row_ids = lax.iota(jnp.int32, shard_piece.shape[0])
    match_table = ((slot_ids[:, None] == row_ids[None, :]) & is_live[:, None]).astype(jnp.float32)
    boundary = jnp.dot(
        match_table, shard_piece, precision=largest_level, preferred_element_type=jnp.float32
    )
    states_low = states.astype(jnp.bfloat16)
    boundary_low = boundary.astype(jnp.bfloat16)
    summed = jnp.einsum(
        "lij,ljr->lir",
        leaf_maps.reshape(leaf_count, node_count, node_count),
        local_loads,
        preferred_element_type=jnp.float32,
    )
    summed = summed + jnp.einsum(
        "lik,kr->lir",
        edge_maps.reshape(leaf_count, node_count, sep_width),
        states_low,
        preferred_element_type=jnp.float32,
    )
    summed = summed + jnp.einsum(
        "lic,cr->lir",
        top_maps.reshape(leaf_count, node_count, slot_total),
        boundary_low,
        preferred_element_type=jnp.float32,
    )
    solution = summed.astype(jnp.bfloat16).reshape(1, 1, 1, leaf_count, node_count, rhs_count)
    return (solution, owned_rows)


def body(sizes, *arrays):
    loads, _, chain_maps, _, _, _, slot_nodes, _, top_loads, top_inverse = arrays
    if fits(sizes, loads, chain_maps, slot_nodes, top_loads, top_inverse):
        return fused_body(sizes, *arrays)
    return plain_body(*arrays)


def solution(mesh):
    sizes = tuple(mesh.shape[axis] for axis in ("leaf", "row", "top"))
    in_specs = (
        P("leaf", "row", "top", None, None, None),
        P("leaf", "row", "top", None, None),
        P("leaf", "row", "top", None, None),
        P("leaf", "row", "top", None, None, None),
        P("leaf", "row", "top", None, None, None),
        P("leaf", "row", "top", None, None, None),
        P("leaf", "row", "top", None),
        P("leaf", "row", "top"),
        P("leaf", None),
        P("top", ("leaf", "row")),
    )
    out_specs = (P("leaf", "row", "top", None, None, None), P("top", None))
    return jax.shard_map(
        functools.partial(body, sizes),
        mesh=mesh,
        in_specs=in_specs,
        out_specs=out_specs,
        check_vma=False,
    )
```

```python
import functools

import jax
import jax.numpy as jnp
from jax import lax
from jax.experimental import pallas as pl
from jax.experimental.pallas import tpu as pltpu
from jax.sharding import PartitionSpec as P

LANES = 128
MESH = pl.DeviceIdType.MESH


def nt(a, b):
    return lax.dot_general(a, b, (((1,), (1,)), ((), ())), preferred_element_type=jnp.float32)


def split(value):
    high = value.astype(jnp.bfloat16)
    low = (value - high.astype(jnp.float32)).astype(jnp.bfloat16)
    return high, low


def fold(value):
    half = value.shape[0] // 2
    return value[:half] + value[half:]


def fused_kernel(
    sizes,
    loads_ref,
    nodes_ref,
    count_ref,
    top_loads_hbm,
    flux_hbm,
    chain_hbm,
    leaf_hbm,
    edge_hbm,
    top_hbm,
    inverse_hbm,
    solution_ref,
    values_hbm,
    top_loads,
    own_ids,
    flux_maps,
    chain,
    leaf_maps,
    edge_maps,
    top_maps,
    inverse,
    chain_high,
    chain_low,
    inverse_high,
    inverse_low,
    fluxes,
    state,
    carry,
    early,
    ids,
    entries,
    scatter_table,
    gather_table,
    rhs,
    partials,
    arrived,
    values,
    picked,
    boundary,
    load_sem,
    carry_send,
    carry_recv,
    id_leaf_send,
    id_leaf_recv,
    id_cell_send,
    id_cell_recv,
    entry_leaf_send,
    entry_leaf_recv,
    entry_cell_send,
    entry_cell_recv,
    part_send,
    part_recv,
    value_send,
    value_recv,
    bound_send,
    bound_recv,
):
    L, R, T = sizes
    cells, owners = R * T, L * R
    leaf, row, top = lax.axis_index("leaf"), lax.axis_index("row"), lax.axis_index("top")
    cell = row * T + top
    owner = leaf * R + row
    nrhs = loads_ref.shape[0]
    slots = nodes_ref.shape[1]
    chunk = inverse.shape[0] // owners
    columns = inverse.shape[1]
    block_rows = inverse.shape[0]

    def along(start, size):
        return pl.ds(pl.multiple_of(start * size, size), size)

    def send(src, dst, send_sem, recv_sem, where):
        return pltpu.make_async_remote_copy(
            src_ref=src,
            dst_ref=dst,
            send_sem=send_sem,
            recv_sem=recv_sem,
            device_id=where,
            device_id_type=MESH,
        )

    def cell_of(step):
        other = lax.rem(cell + step, cells)
        return other, {"row": other // T, "top": lax.rem(other, T)}

    def owner_of(step):
        other = lax.rem(owner + step, owners)
        return other, {"leaf": other // R, "row": lax.rem(other, R)}

    def leaf_of(step):
        other = lax.rem(leaf + step, L)
        return other, {"leaf": other}

    def top_of(step):
        other = lax.rem(top + step, T)
        return other, {"top": other}

    pairs = (
        (flux_hbm, flux_maps),
        (chain_hbm, chain),
        (inverse_hbm, inverse),
        (leaf_hbm, leaf_maps),
        (edge_hbm, edge_maps),
        (top_hbm, top_maps),
        (top_loads_hbm.at[:, along(row, columns)], top_loads),
    )
    fetches = [
        pltpu.make_async_copy(src, dst, load_sem.at[i]) for i, (src, dst) in enumerate(pairs)
    ]
    for fetch in fetches:
        fetch.start()

    barrier = pltpu.get_barrier_semaphore()
    for step in range(1, cells):
        pl.semaphore_signal(barrier, inc=1, device_id=cell_of(step)[1], device_id_type=MESH)
    for step in range(1, owners):
        pl.semaphore_signal(barrier, inc=1, device_id=owner_of(step)[1], device_id_type=MESH)
    live = lax.broadcasted_iota(jnp.int32, own_ids.shape, 1) < count_ref[...]
    own_ids[...] = jnp.where(live, nodes_ref[...], -1)
    mine = cell * L + leaf
    ids[:, along(mine, slots)] = own_ids[...]

    fetches[0].wait()
    fluxes[...] = nt(loads_ref[...], flux_maps[...])
    state[...] = fluxes[...]
    fetches[1].wait()

    @pl.when(leaf > 0)
    def _():
        high, low = split(chain[...])
        chain_high[...] = high
        chain_low[...] = low

    pl.semaphore_wait(barrier, cells + owners - 2)

    id_copies = [
        send(
            own_ids,
            ids.at[:, along(mine, slots)],
            id_leaf_send.at[step - 1],
            id_leaf_recv.at[step - 1],
            leaf_of(step)[1],
        )
        for step in range(1, L)
    ]
    id_cells = [
        send(
            ids.at[:, along(cell, L * slots)],
            ids.at[:, along(cell, L * slots)],
            id_cell_send.at[step - 1],
            id_cell_recv.at[step - 1],
            cell_of(step)[1],
        )
        for step in range(1, cells)
    ]

    def prepare_tables():
        for copy in id_cells:
            copy.wait()

        @pl.loop(0, columns // 32)
        def _(i):
            start = pl.multiple_of(i * 32, 32)
            numbers = lax.broadcasted_iota(jnp.int32, (32, slots), 0) + (owner * columns + start)
            for source in range(L):
                for other in range(cells):
                    wanted = other * L + source
                    place = source * cells + other
                    scatter_table[pl.ds(start, 32), place * slots : (place + 1) * slots] = (
                        jnp.where(
                            numbers == ids[0:1, wanted * slots : (wanted + 1) * slots], 1.0, 0.0
                        ).astype(jnp.bfloat16)
                    )

        @pl.loop(0, block_rows // 64)
        def _(i):
            start = pl.multiple_of(i * 64, 64)
            numbers = lax.broadcasted_iota(jnp.int32, (64, slots), 0) + (top * block_rows + start)
            for other in range(T):
                wanted = ids[0:1, along((row * T + other) * L + leaf, slots)]
                gather_table[pl.ds(start, 64), other * slots : (other + 1) * slots] = jnp.where(
                    numbers == wanted, 1.0, 0.0
                ).astype(jnp.bfloat16)

    def prepare_inverse():
        fetches[2].wait()

        @pl.loop(0, block_rows // 64)
        def _(i):
            start = pl.multiple_of(i * 64, 64)
            high, low = split(inverse[pl.ds(start, 64), :])
            inverse_high[pl.ds(start, 64), :] = high
            inverse_low[pl.ds(start, 64), :] = low

    def entry_leaf(step):
        return send(
            state.at[:, pl.ds(0, slots)],
            entries.at[:, along(leaf * cells + cell, slots)],
            entry_leaf_send.at[step - 1],
            entry_leaf_recv.at[leaf],
            leaf_of(step)[1],
        )

    def entry_landed(source):
        return pltpu.make_async_copy(
            entries.at[:, along(source * cells + cell, slots)],
            entries.at[:, along(source * cells + cell, slots)],
            entry_leaf_recv.at[source],
        )

    def entry_cell(source, step):
        number = source * cells + cell
        return send(
            entries.at[:, along(number, slots)],
            entries.at[:, along(number, slots)],
            entry_cell_send.at[source * cells + step],
            entry_cell_recv.at[number],
            cell_of(step)[1],
        )

    spans = [(at, min(256, fluxes.shape[1] - at)) for at in range(0, fluxes.shape[1], 256)]

    def carry_copy(i):
        part = pl.ds(*spans[i])
        return send(
            state.at[:, part],
            carry.at[:, part],
            carry_send.at[i],
            carry_recv.at[i],
            leaf_of(1)[1],
        )

    def hand_on(i, k):
        @pl.when(k < L - 1)
        def _():
            carry_copy(i).start()

        if i == 0:
            for step in range(1, L):
                entry_leaf(step).start()
            entries[:, along(leaf * cells + cell, slots)] = state[:, :slots]

    def advance(k):
        total = fluxes[...]
        for i, (at, size) in enumerate(spans):
            carry_copy(i).wait_recv()
            high, low = split(carry[:, at : at + size])
            both = jnp.concatenate([high, low], axis=0)
            if i < len(spans) - 1:
                total = (
                    total
                    + fold(nt(both, chain_high[:, at : at + size]))
                    + nt(high, chain_low[:, at : at + size])
                )
                continue
            for j, (to, wide) in enumerate(spans):
                state[:, to : to + wide] = (
                    total[:, to : to + wide]
                    + fold(nt(both, chain_high[to : to + wide, at : at + size]))
                    + nt(high, chain_low[to : to + wide, at : at + size])
                )
                hand_on(j, k)

    def forward(source):
        @pl.when(leaf != source)
        def _():
            entry_landed(source).wait()

        for step in range(1, cells):
            entry_cell(source, step).start()

    @pl.when(leaf == 0)
    def _():
        for j in range(len(spans)):
            hand_on(j, 0)

    for copy in id_copies:
        copy.start()

    @pl.loop(0, L)
    def _(k):
        @pl.when((leaf == k) & (k > 0))
        def _():
            advance(k)

        @pl.when(k > 0)
        def _():
            forward(k - 1)

        @pl.when(k == 1)
        def _():
            for copy in id_copies:
                copy.wait()
            for copy in id_cells:
                copy.start()

        @pl.when(k == 1 - (2 * leaf) // L)
        def _():
            prepare_inverse()

        @pl.when(k == L // 2)
        def _():
            prepare_tables()

    forward(L - 1)

    def gathered_from(source):
        for step in range(1, cells):
            number = source * cells + cell_of(step)[0]
            pltpu.make_async_copy(
                entries.at[:, along(number, slots)],
                entries.at[:, along(number, slots)],
                entry_cell_recv.at[number],
            ).wait()

    fetches[6].wait()
    width = 256
    last = (L - 1) * cells * slots
    for source in range(L - 1):
        gathered_from(source)
    high, low = split(entries[:, :last])
    both = jnp.concatenate([high, low], axis=0)

    @pl.loop(0, columns // width)
    def _(i):
        start = pl.multiple_of(i * width, width)
        top_loads[:, pl.ds(start, width)] = top_loads[:, pl.ds(start, width)] - fold(
            nt(both, scatter_table[pl.ds(start, width), :last])
        )

    gathered_from(L - 1)
    high, low = split(entries[:, last:])
    both_last = jnp.concatenate([high, low], axis=0)

    @pl.loop(0, columns // width)
    def _(i):
        start = pl.multiple_of(i * width, width)
        total = fold(nt(both_last, scatter_table[pl.ds(start, width), last:]))
        high, low = split(top_loads[:, pl.ds(start, width)] - total)
        rhs[0:nrhs, pl.ds(start, width)] = high
        rhs[nrhs : 2 * nrhs, pl.ds(start, width)] = low

    def product(number):
        rows = along(number, chunk)
        return fold(nt(rhs[...], inverse_high[rows, :])) + nt(rhs[0:nrhs, :], inverse_low[rows, :])

    def part_copy(step):
        where = owner_of(step)[1]
        return send(
            partials.at[step],
            arrived.at[step],
            part_send.at[step],
            part_recv.at[step],
            where,
        )

    @pl.loop(1, owners)
    def _(step):
        partials[step] = product(owner_of(step)[0])
        part_copy(step).start()

    total = product(owner)
    for step in range(1, owners):
        part_copy(step).wait_recv()
        total = total + arrived[step]
    values[:, along(owner, chunk)] = total

    def value_copy(step):
        where = owner_of(step)[1]
        return send(
            values.at[:, along(owner, chunk)],
            values.at[:, along(owner, chunk)],
            value_send.at[step],
            value_recv.at[step],
            where,
        )

    for step in range(1, owners):
        value_copy(step).start()
    for fetch in fetches[3:6]:
        fetch.wait()
    early[...] = nt(loads_ref[...], leaf_maps[...]) + nt(
        state[...].astype(jnp.bfloat16), edge_maps[...]
    )
    for step in range(1, owners):
        part_copy(step).wait_send()
    for step in range(1, owners):
        value_copy(step).wait_recv()

    final = values[...]
    write = pltpu.make_async_copy(values, values_hbm, load_sem.at[7])
    write.start()
    gathered = jnp.dot(
        final.astype(jnp.bfloat16), gather_table[...], preferred_element_type=jnp.float32
    )
    for other in range(T):
        picked[other] = gathered[:, other * slots : (other + 1) * slots]

    def bound_copy(step):
        other, where = top_of(step)
        return send(
            picked.at[other], boundary.at[step], bound_send.at[step], bound_recv.at[step], where
        )

    for step in range(1, T):
        bound_copy(step).start()
    bound = picked[top]
    for step in range(1, T):
        bound_copy(step).wait_recv()
        bound = bound + boundary[step]
    late = nt(bound.astype(jnp.bfloat16), top_maps[...])
    solution_ref[...] = (early[...] + late).astype(jnp.bfloat16)

    @pl.when(leaf < L - 1)
    def _():
        for i in range(len(spans)):
            carry_copy(i).wait_send()

    for step in range(1, L):
        entry_leaf(step).wait_send()
    for source in range(L):
        for step in range(1, cells):
            entry_cell(source, step).wait_send()
    write.wait()
    for step in range(1, owners):
        value_copy(step).wait_send()
    for step in range(1, T):
        bound_copy(step).wait_send()


def fused_body(
    sizes,
    loads,
    flux_maps,
    chain_maps,
    leaf_maps,
    edge_maps,
    top_maps,
    slot_nodes,
    slot_counts,
    top_loads,
    top_inverse,
):
    L, R, T = sizes
    cells, owners = R * T, L * R
    node_count, nrhs = loads.shape[4:]
    sep_width = chain_maps.shape[-1]
    slots = slot_nodes.shape[-1]
    block_rows, columns = top_inverse.shape
    chunk = block_rows // owners
    everyone = L * cells
    f32, bf16 = jnp.float32, jnp.bfloat16
    nodes = slot_nodes.reshape(1, slots)
    dma = pltpu.SemaphoreType.DMA
    vmem = pl.BlockSpec(memory_space=pltpu.VMEM)
    anywhere = pl.BlockSpec(memory_space=pl.ANY)
    solution, values = pl.pallas_call(
        functools.partial(fused_kernel, sizes),
        out_shape=(
            jax.ShapeDtypeStruct((nrhs, node_count), bf16),
            jax.ShapeDtypeStruct((nrhs, block_rows), f32),
        ),
        in_specs=[vmem] * 3 + [anywhere] * 7,
        out_specs=(vmem, anywhere),
        scratch_shapes=[
            pltpu.VMEM((nrhs, columns), f32),
            pltpu.VMEM((8, slots), jnp.int32),
            pltpu.VMEM((sep_width, node_count), bf16),
            pltpu.VMEM((sep_width, sep_width), f32),
            pltpu.VMEM((node_count, node_count), bf16),
            pltpu.VMEM((node_count, sep_width), bf16),
            pltpu.VMEM((node_count, slots), bf16),
            pltpu.VMEM((block_rows, columns), f32),
            pltpu.VMEM((sep_width, sep_width), bf16),
            pltpu.VMEM((sep_width, sep_width), bf16),
            pltpu.VMEM((block_rows, columns), bf16),
            pltpu.VMEM((block_rows, columns), bf16),
            pltpu.VMEM((nrhs, sep_width), f32),
            pltpu.VMEM((nrhs, sep_width), f32),
            pltpu.VMEM((nrhs, sep_width), f32),
            pltpu.VMEM((nrhs, node_count), f32),
            pltpu.VMEM((8, everyone * slots), jnp.int32),
            pltpu.VMEM((nrhs, everyone * slots), f32),
            pltpu.VMEM((columns, everyone * slots), bf16),
            pltpu.VMEM((block_rows, T * slots), bf16),
            pltpu.VMEM((2 * nrhs, columns), bf16),
            pltpu.VMEM((owners, nrhs, chunk), f32),
            pltpu.VMEM((owners, nrhs, chunk), f32),
            pltpu.VMEM((nrhs, block_rows), f32),
            pltpu.VMEM((T, nrhs, slots), f32),
            pltpu.VMEM((T, nrhs, slots), f32),
            dma((8,)),
            dma((-(-sep_width // 256),)),
            dma((-(-sep_width // 256),)),
            dma((L,)),
            dma((L,)),
            dma((cells,)),
            dma((cells,)),
            dma((L,)),
            dma((L,)),
            dma((everyone,)),
            dma((everyone,)),
            dma((owners,)),
            dma((owners,)),
            dma((owners,)),
            dma((owners,)),
            dma((T,)),
            dma((T,)),
        ],
        compiler_params=pltpu.CompilerParams(
            collective_id=0, has_side_effects=True, vmem_limit_bytes=56 << 20
        ),
    )(
        loads.reshape(node_count, nrhs).T,
        nodes,
        slot_counts.reshape(1, 1),
        top_loads.T,
        flux_maps.reshape(sep_width, node_count),
        chain_maps.reshape(sep_width, sep_width),
        leaf_maps.reshape(node_count, node_count),
        edge_maps.reshape(node_count, sep_width),
        top_maps.reshape(node_count, slots),
        top_inverse,
    )
    return solution.T.reshape(1, 1, 1, 1, node_count, nrhs), values.T


def fits(sizes, loads, chain_maps, slot_nodes, top_loads, top_inverse):
    L, R, T = sizes
    owners = L * R
    block_rows, columns = top_inverse.shape
    slots = slot_nodes.shape[-1]
    everyone = owners * T * slots
    return (
        min(sizes) > 1
        and loads.shape[3] == 1
        and loads.shape[5] % 16 == 0
        and slots == LANES
        and chain_maps.shape[-1] % LANES == 0
        and loads.shape[4] % LANES == 0
        and columns % 256 == 0
        and block_rows % (owners * LANES) == 0
        and top_loads.shape[0] == R * columns
        and columns * everyone * 2 + block_rows * columns * 8 < (32 << 20)
    )


def passed_along(value, axis, steps):
    count = lax.axis_size(axis)
    first, last = (max(0, -steps), min(count, count - steps))
    return lax.ppermute(value, axis, [(source, source + steps) for source in range(first, last)])


def plain_body(
    loads,
    flux_maps,
    chain_maps,
    leaf_maps,
    edge_maps,
    top_maps,
    slot_nodes,
    slot_counts,
    top_loads,
    top_inverse,
):
    leaf_count = loads.shape[3]
    node_count = loads.shape[4]
    rhs_count = loads.shape[5]
    sep_width = chain_maps.shape[-1]
    slot_total = slot_nodes.shape[-1]
    largest_level = lax.Precision.HIGHEST
    local_loads = loads.reshape(leaf_count, node_count, rhs_count)
    flattened = loads.reshape(leaf_count * node_count, rhs_count)
    fluxes = jnp.dot(
        flux_maps.reshape(sep_width, leaf_count * node_count),
        flattened,
        preferred_element_type=jnp.float32,
    )
    combine_operator = chain_maps.reshape(sep_width, sep_width)
    chain_index = lax.axis_index("leaf")

    def advance(step_index, carried):
        earlier = passed_along(carried, "leaf", 1)
        advanced = (
            jnp.dot(
                combine_operator,
                earlier,
                precision=largest_level,
                preferred_element_type=jnp.float32,
            )
            + fluxes
        )
        return jnp.where(chain_index == step_index, advanced, carried)

    states = lax.fori_loop(1, lax.axis_size("leaf"), advance, fluxes)
    slot_ids = slot_nodes.reshape(slot_total)
    is_live = lax.iota(jnp.int32, slot_total) < slot_counts.reshape(())
    chosen_entries = jnp.where(is_live[:, None], states[:slot_total], jnp.float32(0.0))
    block_rows = top_loads.shape[0]
    row_ids = lax.iota(jnp.int32, block_rows * lax.axis_size("leaf"))
    match_table = (row_ids[:, None] == slot_ids[None, :]).astype(jnp.float32)
    top_block = lax.psum_scatter(
        jnp.dot(
            match_table, chosen_entries, precision=largest_level, preferred_element_type=jnp.float32
        ),
        "leaf",
        scatter_dimension=0,
        tiled=True,
    )
    top_block = lax.psum(top_block, ("row", "top"))
    rhs_block = top_loads - top_block
    column_rows = top_inverse.shape[1]
    rhs_piece = lax.dynamic_slice_in_dim(
        rhs_block, lax.axis_index("row") * column_rows, column_rows, 0
    )
    partial_value = jnp.dot(
        top_inverse, rhs_piece, precision=largest_level, preferred_element_type=jnp.float32
    )
    owned_rows = lax.psum(partial_value, ("leaf", "row"))
    shard_piece = lax.all_gather(owned_rows, "top", axis=0, tiled=True)
    row_ids = lax.iota(jnp.int32, shard_piece.shape[0])
    match_table = ((slot_ids[:, None] == row_ids[None, :]) & is_live[:, None]).astype(jnp.float32)
    boundary = jnp.dot(
        match_table, shard_piece, precision=largest_level, preferred_element_type=jnp.float32
    )
    states_low = states.astype(jnp.bfloat16)
    boundary_low = boundary.astype(jnp.bfloat16)
    summed = jnp.einsum(
        "lij,ljr->lir",
        leaf_maps.reshape(leaf_count, node_count, node_count),
        local_loads,
        preferred_element_type=jnp.float32,
    )
    summed = summed + jnp.einsum(
        "lik,kr->lir",
        edge_maps.reshape(leaf_count, node_count, sep_width),
        states_low,
        preferred_element_type=jnp.float32,
    )
    summed = summed + jnp.einsum(
        "lic,cr->lir",
        top_maps.reshape(leaf_count, node_count, slot_total),
        boundary_low,
        preferred_element_type=jnp.float32,
    )
    solution = summed.astype(jnp.bfloat16).reshape(1, 1, 1, leaf_count, node_count, rhs_count)
    return (solution, owned_rows)


def body(sizes, *arrays):
    loads, _, chain_maps, _, _, _, slot_nodes, _, top_loads, top_inverse = arrays
    if fits(sizes, loads, chain_maps, slot_nodes, top_loads, top_inverse):
        return fused_body(sizes, *arrays)
    return plain_body(*arrays)


def solution(mesh):
    sizes = tuple(mesh.shape[axis] for axis in ("leaf", "row", "top"))
    in_specs = (
        P("leaf", "row", "top", None, None, None),
        P("leaf", "row", "top", None, None),
        P("leaf", "row", "top", None, None),
        P("leaf", "row", "top", None, None, None),
        P("leaf", "row", "top", None, None, None),
        P("leaf", "row", "top", None, None, None),
        P("leaf", "row", "top", None),
        P("leaf", "row", "top"),
        P("leaf", None),
        P("top", ("leaf", "row")),
    )
    out_specs = (P("leaf", "row", "top", None, None, None), P("top", None))
    return jax.shard_map(
        functools.partial(body, sizes),
        mesh=mesh,
        in_specs=in_specs,
        out_specs=out_specs,
        check_vma=False,
    )
```

```python
import functools

import jax
import jax.numpy as jnp
from jax import lax
from jax.experimental import pallas as pl
from jax.experimental.pallas import tpu as pltpu
from jax.sharding import PartitionSpec as P

LANES = 128
MESH = pl.DeviceIdType.MESH


def nt(a, b):
    return lax.dot_general(a, b, (((1,), (1,)), ((), ())), preferred_element_type=jnp.float32)


def split(value):
    high = value.astype(jnp.bfloat16)
    low = (value - high.astype(jnp.float32)).astype(jnp.bfloat16)
    return high, low


def fold(value):
    half = value.shape[0] // 2
    return value[:half] + value[half:]


def fused_kernel(
    sizes,
    loads_ref,
    nodes_ref,
    count_ref,
    top_loads_hbm,
    flux_hbm,
    chain_hbm,
    leaf_hbm,
    edge_hbm,
    top_hbm,
    inverse_hbm,
    solution_ref,
    values_hbm,
    top_loads,
    own_ids,
    flux_maps,
    chain,
    leaf_maps,
    edge_maps,
    top_maps,
    inverse,
    chain_high,
    chain_low,
    inverse_high,
    inverse_low,
    fluxes,
    state,
    carry,
    early,
    ids,
    entries,
    scatter_table,
    gather_table,
    rhs,
    partials,
    arrived,
    values,
    picked,
    boundary,
    load_sem,
    carry_send,
    carry_recv,
    id_leaf_send,
    id_leaf_recv,
    id_cell_send,
    id_cell_recv,
    entry_leaf_send,
    entry_leaf_recv,
    entry_cell_send,
    entry_cell_recv,
    part_send,
    part_recv,
    value_send,
    value_recv,
    bound_send,
    bound_recv,
):
    L, R, T = sizes
    cells, owners = R * T, L * R
    leaf, row, top = lax.axis_index("leaf"), lax.axis_index("row"), lax.axis_index("top")
    cell = row * T + top
    owner = leaf * R + row
    nrhs = loads_ref.shape[0]
    slots = nodes_ref.shape[1]
    chunk = inverse.shape[0] // owners
    columns = inverse.shape[1]
    block_rows = inverse.shape[0]

    def along(start, size):
        return pl.ds(pl.multiple_of(start * size, size), size)

    def send(src, dst, send_sem, recv_sem, where):
        return pltpu.make_async_remote_copy(
            src_ref=src,
            dst_ref=dst,
            send_sem=send_sem,
            recv_sem=recv_sem,
            device_id=where,
            device_id_type=MESH,
        )

    def cell_of(step):
        other = lax.rem(cell + step, cells)
        return other, {"row": other // T, "top": lax.rem(other, T)}

    def owner_of(step):
        other = lax.rem(owner + step, owners)
        return other, {"leaf": other // R, "row": lax.rem(other, R)}

    def leaf_of(step):
        other = lax.rem(leaf + step, L)
        return other, {"leaf": other}

    def top_of(step):
        other = lax.rem(top + step, T)
        return other, {"top": other}

    pairs = (
        (flux_hbm, flux_maps),
        (chain_hbm, chain),
        (inverse_hbm, inverse),
        (leaf_hbm, leaf_maps),
        (edge_hbm, edge_maps),
        (top_hbm, top_maps),
        (top_loads_hbm.at[:, along(row, columns)], top_loads),
    )
    fetches = [
        pltpu.make_async_copy(src, dst, load_sem.at[i]) for i, (src, dst) in enumerate(pairs)
    ]
    for fetch in fetches:
        fetch.start()

    barrier = pltpu.get_barrier_semaphore()
    for step in range(1, cells):
        pl.semaphore_signal(barrier, inc=1, device_id=cell_of(step)[1], device_id_type=MESH)
    for step in range(1, owners):
        pl.semaphore_signal(barrier, inc=1, device_id=owner_of(step)[1], device_id_type=MESH)
    live = lax.broadcasted_iota(jnp.int32, own_ids.shape, 1) < count_ref[...]
    own_ids[...] = jnp.where(live, nodes_ref[...], -1)
    mine = cell * L + leaf
    ids[:, along(mine, slots)] = own_ids[...]

    fetches[0].wait()
    fluxes[...] = nt(loads_ref[...], flux_maps[...])
    state[...] = fluxes[...]
    fetches[1].wait()

    @pl.when(leaf > 0)
    def _():
        high, low = split(chain[...])
        chain_high[...] = high
        chain_low[...] = low

    pl.semaphore_wait(barrier, cells + owners - 2)

    id_copies = [
        send(
            own_ids,
            ids.at[:, along(mine, slots)],
            id_leaf_send.at[step - 1],
            id_leaf_recv.at[step - 1],
            leaf_of(step)[1],
        )
        for step in range(1, L)
    ]
    id_cells = [
        send(
            ids.at[:, along(cell, L * slots)],
            ids.at[:, along(cell, L * slots)],
            id_cell_send.at[step - 1],
            id_cell_recv.at[step - 1],
            cell_of(step)[1],
        )
        for step in range(1, cells)
    ]

    def prepare_tables():
        for copy in id_cells:
            copy.wait()

        @pl.loop(0, columns // 32)
        def _(i):
            start = pl.multiple_of(i * 32, 32)
            numbers = lax.broadcasted_iota(jnp.int32, (32, slots), 0) + (owner * columns + start)
            for source in range(L):
                for other in range(cells):
                    wanted = other * L + source
                    place = source * cells + other
                    scatter_table[pl.ds(start, 32), place * slots : (place + 1) * slots] = (
                        jnp.where(
                            numbers == ids[0:1, wanted * slots : (wanted + 1) * slots], 1.0, 0.0
                        ).astype(jnp.bfloat16)
                    )

        @pl.loop(0, block_rows // 64)
        def _(i):
            start = pl.multiple_of(i * 64, 64)
            numbers = lax.broadcasted_iota(jnp.int32, (64, slots), 0) + (top * block_rows + start)
            for other in range(T):
                wanted = ids[0:1, along((row * T + other) * L + leaf, slots)]
                gather_table[pl.ds(start, 64), other * slots : (other + 1) * slots] = jnp.where(
                    numbers == wanted, 1.0, 0.0
                ).astype(jnp.bfloat16)

    def prepare_inverse():
        fetches[2].wait()

        @pl.loop(0, block_rows // 64)
        def _(i):
            start = pl.multiple_of(i * 64, 64)
            high, low = split(inverse[pl.ds(start, 64), :])
            inverse_high[pl.ds(start, 64), :] = high
            inverse_low[pl.ds(start, 64), :] = low

    def entry_leaf(step):
        return send(
            state.at[:, pl.ds(0, slots)],
            entries.at[:, along(leaf * cells + cell, slots)],
            entry_leaf_send.at[step - 1],
            entry_leaf_recv.at[leaf],
            leaf_of(step)[1],
        )

    def entry_landed(source):
        return pltpu.make_async_copy(
            entries.at[:, along(source * cells + cell, slots)],
            entries.at[:, along(source * cells + cell, slots)],
            entry_leaf_recv.at[source],
        )

    def entry_cell(source, step):
        number = source * cells + cell
        return send(
            entries.at[:, along(number, slots)],
            entries.at[:, along(number, slots)],
            entry_cell_send.at[source * cells + step],
            entry_cell_recv.at[number],
            cell_of(step)[1],
        )

    spans = [(at, min(256, fluxes.shape[1] - at)) for at in range(0, fluxes.shape[1], 256)]

    def carry_copy(i):
        part = pl.ds(*spans[i])
        return send(
            state.at[:, part],
            carry.at[:, part],
            carry_send.at[i],
            carry_recv.at[i],
            leaf_of(1)[1],
        )

    def hand_on(i, k):
        @pl.when(k < L - 1)
        def _():
            carry_copy(i).start()

        if i == 0:
            for step in range(1, L):
                entry_leaf(step).start()
            entries[:, along(leaf * cells + cell, slots)] = state[:, :slots]

    def advance(k):
        total = fluxes[...]
        for i, (at, size) in enumerate(spans):
            carry_copy(i).wait_recv()
            high, low = split(carry[:, at : at + size])
            both = jnp.concatenate([high, low], axis=0)
            if i < len(spans) - 1:
                total = (
                    total
                    + fold(nt(both, chain_high[:, at : at + size]))
                    + nt(high, chain_low[:, at : at + size])
                )
                continue
            for j, (to, wide) in enumerate(spans):
                state[:, to : to + wide] = (
                    total[:, to : to + wide]
                    + fold(nt(both, chain_high[to : to + wide, at : at + size]))
                    + nt(high, chain_low[to : to + wide, at : at + size])
                )
                hand_on(j, k)

    def forward(source):
        @pl.when(leaf != source)
        def _():
            entry_landed(source).wait()

        for step in range(1, cells):
            entry_cell(source, step).start()

    @pl.when(leaf == 0)
    def _():
        for j in range(len(spans)):
            hand_on(j, 0)

    for copy in id_copies:
        copy.start()

    @pl.loop(0, L)
    def _(k):
        @pl.when((leaf == k) & (k > 0))
        def _():
            advance(k)

        @pl.when(k > 0)
        def _():
            forward(k - 1)

        @pl.when(k == 1)
        def _():
            for copy in id_copies:
                copy.wait()
            for copy in id_cells:
                copy.start()

        @pl.when(k == 1 - (2 * leaf) // L)
        def _():
            prepare_inverse()

        @pl.when(k == L // 2)
        def _():
            prepare_tables()

    forward(L - 1)

    def gathered_from(source):
        for step in range(1, cells):
            number = source * cells + cell_of(step)[0]
            pltpu.make_async_copy(
                entries.at[:, along(number, slots)],
                entries.at[:, along(number, slots)],
                entry_cell_recv.at[number],
            ).wait()

    fetches[6].wait()
    width = 256
    last = (L - 1) * cells * slots
    for source in range(L - 1):
        gathered_from(source)
    high, low = split(entries[:, :last])
    both = jnp.concatenate([high, low], axis=0)

    @pl.loop(0, columns // width)
    def _(i):
        start = pl.multiple_of(i * width, width)
        top_loads[:, pl.ds(start, width)] = top_loads[:, pl.ds(start, width)] - fold(
            nt(both, scatter_table[pl.ds(start, width), :last])
        )

    gathered_from(L - 1)
    high, low = split(entries[:, last:])
    both_last = jnp.concatenate([high, low], axis=0)

    @pl.loop(0, columns // width)
    def _(i):
        start = pl.multiple_of(i * width, width)
        total = fold(nt(both_last, scatter_table[pl.ds(start, width), last:]))
        high, low = split(top_loads[:, pl.ds(start, width)] - total)
        rhs[0:nrhs, pl.ds(start, width)] = high
        rhs[nrhs : 2 * nrhs, pl.ds(start, width)] = low

    def product(number):
        rows = along(number, chunk)
        return fold(nt(rhs[...], inverse_high[rows, :])) + nt(rhs[0:nrhs, :], inverse_low[rows, :])

    def part_copy(step):
        where = owner_of(step)[1]
        return send(
            partials.at[step],
            arrived.at[step],
            part_send.at[step],
            part_recv.at[step],
            where,
        )

    half = owners // 2

    @pl.loop(0, owners - 1)
    def _(i):
        step = jnp.where(i < half, 2 * i + 1, 2 * (i - half) + 2)
        partials[step] = product(owner_of(step)[0])
        part_copy(step).start()

    total = product(owner)
    for step in range(1, owners):
        part_copy(step).wait_recv()
        total = total + arrived[step]
    values[:, along(owner, chunk)] = total

    def value_copy(step):
        where = owner_of(step)[1]
        return send(
            values.at[:, along(owner, chunk)],
            values.at[:, along(owner, chunk)],
            value_send.at[step],
            value_recv.at[step],
            where,
        )

    for step in range(1, owners):
        value_copy(step).start()
    for fetch in fetches[3:6]:
        fetch.wait()
    early[...] = nt(loads_ref[...], leaf_maps[...]) + nt(
        state[...].astype(jnp.bfloat16), edge_maps[...]
    )
    for step in range(1, owners):
        part_copy(step).wait_send()
    for step in range(1, owners):
        value_copy(step).wait_recv()

    final = values[...]
    write = pltpu.make_async_copy(values, values_hbm, load_sem.at[7])
    write.start()
    gathered = jnp.dot(
        final.astype(jnp.bfloat16), gather_table[...], preferred_element_type=jnp.float32
    )
    for other in range(T):
        picked[other] = gathered[:, other * slots : (other + 1) * slots]

    def bound_copy(step):
        other, where = top_of(step)
        return send(
            picked.at[other], boundary.at[step], bound_send.at[step], bound_recv.at[step], where
        )

    for step in range(1, T):
        bound_copy(step).start()
    bound = picked[top]
    for step in range(1, T):
        bound_copy(step).wait_recv()
        bound = bound + boundary[step]
    late = nt(bound.astype(jnp.bfloat16), top_maps[...])
    solution_ref[...] = (early[...] + late).astype(jnp.bfloat16)

    @pl.when(leaf < L - 1)
    def _():
        for i in range(len(spans)):
            carry_copy(i).wait_send()

    for step in range(1, L):
        entry_leaf(step).wait_send()
    for source in range(L):
        for step in range(1, cells):
            entry_cell(source, step).wait_send()
    write.wait()
    for step in range(1, owners):
        value_copy(step).wait_send()
    for step in range(1, T):
        bound_copy(step).wait_send()


def finish_kernel(solution_ref, values_ref, solution_out, values_out):
    solution_out[...] = solution_ref[...]
    values_out[...] = values_ref[...]


def fused_body(
    sizes,
    loads,
    flux_maps,
    chain_maps,
    leaf_maps,
    edge_maps,
    top_maps,
    slot_nodes,
    slot_counts,
    top_loads,
    top_inverse,
):
    L, R, T = sizes
    cells, owners = R * T, L * R
    node_count, nrhs = loads.shape[4:]
    sep_width = chain_maps.shape[-1]
    slots = slot_nodes.shape[-1]
    block_rows, columns = top_inverse.shape
    chunk = block_rows // owners
    everyone = L * cells
    f32, bf16 = jnp.float32, jnp.bfloat16
    nodes = slot_nodes.reshape(1, slots)
    dma = pltpu.SemaphoreType.DMA
    vmem = pl.BlockSpec(memory_space=pltpu.VMEM)
    anywhere = pl.BlockSpec(memory_space=pl.ANY)
    solution, values = pl.pallas_call(
        functools.partial(fused_kernel, sizes),
        out_shape=(
            jax.ShapeDtypeStruct((nrhs, node_count), bf16),
            jax.ShapeDtypeStruct((nrhs, block_rows), f32),
        ),
        in_specs=[vmem] * 3 + [anywhere] * 7,
        out_specs=(vmem, anywhere),
        scratch_shapes=[
            pltpu.VMEM((nrhs, columns), f32),
            pltpu.VMEM((8, slots), jnp.int32),
            pltpu.VMEM((sep_width, node_count), bf16),
            pltpu.VMEM((sep_width, sep_width), f32),
            pltpu.VMEM((node_count, node_count), bf16),
            pltpu.VMEM((node_count, sep_width), bf16),
            pltpu.VMEM((node_count, slots), bf16),
            pltpu.VMEM((block_rows, columns), f32),
            pltpu.VMEM((sep_width, sep_width), bf16),
            pltpu.VMEM((sep_width, sep_width), bf16),
            pltpu.VMEM((block_rows, columns), bf16),
            pltpu.VMEM((block_rows, columns), bf16),
            pltpu.VMEM((nrhs, sep_width), f32),
            pltpu.VMEM((nrhs, sep_width), f32),
            pltpu.VMEM((nrhs, sep_width), f32),
            pltpu.VMEM((nrhs, node_count), f32),
            pltpu.VMEM((8, everyone * slots), jnp.int32),
            pltpu.VMEM((nrhs, everyone * slots), f32),
            pltpu.VMEM((columns, everyone * slots), bf16),
            pltpu.VMEM((block_rows, T * slots), bf16),
            pltpu.VMEM((2 * nrhs, columns), bf16),
            pltpu.VMEM((owners, nrhs, chunk), f32),
            pltpu.VMEM((owners, nrhs, chunk), f32),
            pltpu.VMEM((nrhs, block_rows), f32),
            pltpu.VMEM((T, nrhs, slots), f32),
            pltpu.VMEM((T, nrhs, slots), f32),
            dma((8,)),
            dma((-(-sep_width // 256),)),
            dma((-(-sep_width // 256),)),
            dma((L,)),
            dma((L,)),
            dma((cells,)),
            dma((cells,)),
            dma((L,)),
            dma((L,)),
            dma((everyone,)),
            dma((everyone,)),
            dma((owners,)),
            dma((owners,)),
            dma((owners,)),
            dma((owners,)),
            dma((T,)),
            dma((T,)),
        ],
        compiler_params=pltpu.CompilerParams(
            collective_id=0, has_side_effects=True, vmem_limit_bytes=56 << 20
        ),
    )(
        loads.reshape(node_count, nrhs).T,
        nodes,
        slot_counts.reshape(1, 1),
        top_loads.T,
        flux_maps.reshape(sep_width, node_count),
        chain_maps.reshape(sep_width, sep_width),
        leaf_maps.reshape(node_count, node_count),
        edge_maps.reshape(node_count, sep_width),
        top_maps.reshape(node_count, slots),
        top_inverse,
    )
    solution, values = pl.pallas_call(
        finish_kernel,
        out_shape=(
            jax.ShapeDtypeStruct(solution.shape, solution.dtype),
            jax.ShapeDtypeStruct(values.shape, values.dtype),
        ),
        in_specs=[vmem, vmem],
        out_specs=(vmem, vmem),
    )(solution, values)
    return solution.T.reshape(1, 1, 1, 1, node_count, nrhs), values.T


def fits(sizes, loads, chain_maps, slot_nodes, top_loads, top_inverse):
    L, R, T = sizes
    owners = L * R
    block_rows, columns = top_inverse.shape
    slots = slot_nodes.shape[-1]
    everyone = owners * T * slots
    return (
        min(sizes) > 1
        and loads.shape[3] == 1
        and loads.shape[5] % 16 == 0
        and slots == LANES
        and chain_maps.shape[-1] % LANES == 0
        and loads.shape[4] % LANES == 0
        and columns % 256 == 0
        and block_rows % (owners * LANES) == 0
        and top_loads.shape[0] == R * columns
        and columns * everyone * 2 + block_rows * columns * 8 < (32 << 20)
    )


def passed_along(value, axis, steps):
    count = lax.axis_size(axis)
    first, last = (max(0, -steps), min(count, count - steps))
    return lax.ppermute(value, axis, [(source, source + steps) for source in range(first, last)])


def plain_body(
    loads,
    flux_maps,
    chain_maps,
    leaf_maps,
    edge_maps,
    top_maps,
    slot_nodes,
    slot_counts,
    top_loads,
    top_inverse,
):
    leaf_count = loads.shape[3]
    node_count = loads.shape[4]
    rhs_count = loads.shape[5]
    sep_width = chain_maps.shape[-1]
    slot_total = slot_nodes.shape[-1]
    largest_level = lax.Precision.HIGHEST
    local_loads = loads.reshape(leaf_count, node_count, rhs_count)
    flattened = loads.reshape(leaf_count * node_count, rhs_count)
    fluxes = jnp.dot(
        flux_maps.reshape(sep_width, leaf_count * node_count),
        flattened,
        preferred_element_type=jnp.float32,
    )
    combine_operator = chain_maps.reshape(sep_width, sep_width)
    chain_index = lax.axis_index("leaf")

    def advance(step_index, carried):
        earlier = passed_along(carried, "leaf", 1)
        advanced = (
            jnp.dot(
                combine_operator,
                earlier,
                precision=largest_level,
                preferred_element_type=jnp.float32,
            )
            + fluxes
        )
        return jnp.where(chain_index == step_index, advanced, carried)

    states = lax.fori_loop(1, lax.axis_size("leaf"), advance, fluxes)
    slot_ids = slot_nodes.reshape(slot_total)
    is_live = lax.iota(jnp.int32, slot_total) < slot_counts.reshape(())
    chosen_entries = jnp.where(is_live[:, None], states[:slot_total], jnp.float32(0.0))
    block_rows = top_loads.shape[0]
    row_ids = lax.iota(jnp.int32, block_rows * lax.axis_size("leaf"))
    match_table = (row_ids[:, None] == slot_ids[None, :]).astype(jnp.float32)
    top_block = lax.psum_scatter(
        jnp.dot(
            match_table, chosen_entries, precision=largest_level, preferred_element_type=jnp.float32
        ),
        "leaf",
        scatter_dimension=0,
        tiled=True,
    )
    top_block = lax.psum(top_block, ("row", "top"))
    rhs_block = top_loads - top_block
    column_rows = top_inverse.shape[1]
    rhs_piece = lax.dynamic_slice_in_dim(
        rhs_block, lax.axis_index("row") * column_rows, column_rows, 0
    )
    partial_value = jnp.dot(
        top_inverse, rhs_piece, precision=largest_level, preferred_element_type=jnp.float32
    )
    owned_rows = lax.psum(partial_value, ("leaf", "row"))
    shard_piece = lax.all_gather(owned_rows, "top", axis=0, tiled=True)
    row_ids = lax.iota(jnp.int32, shard_piece.shape[0])
    match_table = ((slot_ids[:, None] == row_ids[None, :]) & is_live[:, None]).astype(jnp.float32)
    boundary = jnp.dot(
        match_table, shard_piece, precision=largest_level, preferred_element_type=jnp.float32
    )
    states_low = states.astype(jnp.bfloat16)
    boundary_low = boundary.astype(jnp.bfloat16)
    summed = jnp.einsum(
        "lij,ljr->lir",
        leaf_maps.reshape(leaf_count, node_count, node_count),
        local_loads,
        preferred_element_type=jnp.float32,
    )
    summed = summed + jnp.einsum(
        "lik,kr->lir",
        edge_maps.reshape(leaf_count, node_count, sep_width),
        states_low,
        preferred_element_type=jnp.float32,
    )
    summed = summed + jnp.einsum(
        "lic,cr->lir",
        top_maps.reshape(leaf_count, node_count, slot_total),
        boundary_low,
        preferred_element_type=jnp.float32,
    )
    solution = summed.astype(jnp.bfloat16).reshape(1, 1, 1, leaf_count, node_count, rhs_count)
    return (solution, owned_rows)


def body(sizes, *arrays):
    loads, _, chain_maps, _, _, _, slot_nodes, _, top_loads, top_inverse = arrays
    if fits(sizes, loads, chain_maps, slot_nodes, top_loads, top_inverse):
        return fused_body(sizes, *arrays)
    return plain_body(*arrays)


def solution(mesh):
    sizes = tuple(mesh.shape[axis] for axis in ("leaf", "row", "top"))
    in_specs = (
        P("leaf", "row", "top", None, None, None),
        P("leaf", "row", "top", None, None),
        P("leaf", "row", "top", None, None),
        P("leaf", "row", "top", None, None, None),
        P("leaf", "row", "top", None, None, None),
        P("leaf", "row", "top", None, None, None),
        P("leaf", "row", "top", None),
        P("leaf", "row", "top"),
        P("leaf", None),
        P("top", ("leaf", "row")),
    )
    out_specs = (P("leaf", "row", "top", None, None, None), P("top", None))
    return jax.shard_map(
        functools.partial(body, sizes),
        mesh=mesh,
        in_specs=in_specs,
        out_specs=out_specs,
        check_vma=False,
    )
```
